32 devices in a mesh: cls: 4 (over x, core), draw: 8 (over z, y).
Axes of the slice: x: 2, y: 2, z: 4, core: 2. Of those that a mesh axis runs over, the one named last changes fastest.
Arguments:
- features: bfloat16 [128, 1024], replicated, may hold values from -128 to 128
- mean_head: bfloat16 [1024, 21888], P('draw', 'cls'), may hold values from -1 to 1
- scale_head: bfloat16 [1024, 21888], P('draw', 'cls'), may hold values from -1 to 1
- factor: bfloat16 [21888, 50], P('cls'), may hold values from -0.875 to 0.875
- noise: bfloat16 [16, 128, 50], P('draw'), may hold values from -5 to 5
- labels: float32 [128, 21888], P(None, 'cls'), may hold values from 0 to 1, as said below
Outputs:
- mean_grad: float32 [1024, 21888], P('draw', 'cls')
- scale_grad: float32 [1024, 21888], P('draw', 'cls')
- feature_grad: float32 [128, 1024], P(None, 'draw')
The draws below stay inside these ranges and needn't reach their ends.
Inputs may be any that keep to these rules, and one draw needn't show every extreme that they name: `labels`: each row is nonnegative, sums to one, and is zero on the last 45 classes.
All inputs are finite; a program needn't handle non-finite values.
Results may differ from the reference program's by a relative error of at most 0.0028.
Values may be sent and summed in bfloat16 or wider, within the bound.
A program may use at most 320 MiB of HBM per device.

```python
import math
import jax
import jax.numpy as jnp
from jax import lax

B = 128
D = 1024
C = 21888
R = 50
CREAL = 21843
S = 16


def head_pair(key):
    norm_scale = 1.0 / math.sqrt(D)
    mean_weight = jax.random.truncated_normal(jax.random.fold_in(key, 11), -6.0, 6.0, (D, C), jnp.float32) * norm_scale
    scale_weight = jax.random.truncated_normal(jax.random.fold_in(key, 12), -6.0, 6.0, (D, C), jnp.float32) * norm_scale
    return (mean_weight.astype(jnp.bfloat16), scale_weight.astype(jnp.bfloat16))


def draw_mean_head(key, part):
    return head_pair(key)[0]


def draw_scale_head(key, part):
    return head_pair(key)[1]


def draw_features(key, part):
    return jax.random.truncated_normal(jax.random.fold_in(key, 20), -6.0, 6.0, (B, D), jnp.float32).astype(jnp.bfloat16)


def draw_labels(key, part):
    logits = 2.0 * jax.random.normal(key, (B, C), jnp.float32)
    valid = jnp.arange(C) < CREAL
    weights = jnp.where(valid[None, :], jnp.exp(logits - jnp.max(logits, axis=1, keepdims=True)), 0.0)
    return (weights / jnp.sum(weights, axis=1, keepdims=True)).astype(jnp.float32)


def levels(rng, extent, cuts, smallest, high):
    gain, own = 1.0, jax.random.fold_in(rng, 6)
    for position, blocks in cuts:
        heights = jnp.exp(jax.random.uniform(jax.random.fold_in(own, position), (blocks,), jnp.float32, smallest / len(cuts), high / len(cuts)))
        gain = gain * jnp.repeat(heights, extent[position] // blocks).reshape([-1 if axis == position else 1 for axis in range(len(extent))])
    return gain


def scatter_about(stream_key, dims, scale, bound, cuts=(), held_as=jnp.bfloat16):
    entries = scale * jax.random.normal(stream_key, dims, jnp.float32)
    if cuts:
        entries = entries * levels(stream_key, dims, cuts, -0.22, 0.18)
    return jnp.clip(entries, -bound, bound).astype(held_as)


def setup_inputs(seed: int = 0) -> dict:
    arg_keys = jax.random.split(jax.random.key(seed), 7)
    features = draw_features(jax.random.fold_in(arg_keys[6], 71), 0)
    mean_head = draw_mean_head(jax.random.fold_in(arg_keys[6], 71), 0)
    scale_head = draw_scale_head(jax.random.fold_in(arg_keys[6], 71), 0)
    factor = scatter_about(arg_keys[3], (C, R), R ** -0.5, 0.875, ((0, 4),))
    noise = scatter_about(arg_keys[4], (S, B, R), 1.0, 5.0, ((0, 8),))
    labels = draw_labels(jax.random.fold_in(arg_keys[6], 71), 0)
    return dict(features=features, mean_head=mean_head, scale_head=scale_head, factor=factor, noise=noise, labels=labels)


def reference(features, mean_head, scale_head, factor, noise, labels):
    mean_logit = jnp.dot(features.astype(jnp.float32), mean_head.astype(jnp.float32), preferred_element_type=jnp.float32)
    scale_pre = jnp.dot(features.astype(jnp.float32), scale_head.astype(jnp.float32), preferred_element_type=jnp.float32)
    spread = jax.nn.softplus(scale_pre)
    class_ids = jnp.arange(C, dtype=jnp.int32)
    shift = jnp.where(class_ids >= CREAL, 30000.0, 0.0).astype(jnp.float32)
    factor_t = factor.T

    def noisy(sample):
        lowrank = jnp.dot(sample.astype(jnp.float32), factor_t.astype(jnp.float32), preferred_element_type=jnp.float32)
        return (lowrank, mean_logit + spread * lowrank - shift[None, :])

    def logprob(sample):
        lowrank, logits = noisy(sample)
        row_max = jnp.max(logits, axis=1)
        total = jnp.sum(jnp.exp(logits - row_max[:, None]), axis=1)
        return (lowrank, logits - (row_max + jnp.log(total))[:, None])

    def first_pass(carry, sample):
        best, summed = carry
        lowrank, logp = logprob(sample)
        top = jnp.maximum(best, logp)
        summed = summed * jnp.exp(best - top) + jnp.exp(logp - top)
        return ((top, summed), None)
    start = (jnp.full((B, C), -jnp.inf, jnp.float32), jnp.zeros((B, C), jnp.float32))
    (best, summed), _ = lax.scan(first_pass, start, noise)
    mix = best + jnp.log(summed)

    def second_pass(carry, sample):
        dmean, dspread = carry
        lowrank, logp = logprob(sample)
        ratio = jnp.exp(logp - mix)
        dots = jnp.sum(labels * ratio, axis=1)
        dz = (jnp.exp(logp) * dots[:, None] - labels * ratio) / B
        return ((dmean + dz, dspread + dz * lowrank), None)
    zeros = jnp.zeros((B, C), jnp.float32)
    (dmean, dspread), _ = lax.scan(second_pass, (zeros, zeros), noise)
    mean_cot = dmean.astype(jnp.bfloat16)
    scale_cot = (dspread * jax.nn.sigmoid(scale_pre)).astype(jnp.bfloat16)
    mean_grad = jnp.dot(features.T.astype(jnp.float32), mean_cot.astype(jnp.float32), preferred_element_type=jnp.float32)
    scale_grad = jnp.dot(features.T.astype(jnp.float32), scale_cot.astype(jnp.float32), preferred_element_type=jnp.float32)
    feature_grad = jnp.dot(mean_cot.astype(jnp.float32), mean_head.T.astype(jnp.float32), preferred_element_type=jnp.float32) + jnp.dot(scale_cot.astype(jnp.float32), scale_head.T.astype(jnp.float32), preferred_element_type=jnp.float32)
    return (mean_grad, scale_grad, feature_grad)
```

```python
import functools
import jax
import jax.numpy as jnp
from jax import lax
from jax.experimental import pallas as pl
from jax.experimental.pallas import tpu as pltpu
from jax.sharding import PartitionSpec as P

CREAL = 21843
MESH = pl.DeviceIdType.MESH
ANY = pl.BlockSpec(memory_space=pl.ANY)
VMEM = pl.BlockSpec(memory_space=pltpu.VMEM)


def at_width(owner, full, part, tile, run):
    @pl.when(owner < full)
    def _():
        run(tile)

    if part:

        @pl.when(owner == full)
        def _():
            run(part)


def exchange_kernel(n, tile, full, part, mean, scale, noise, out, noise_out, send, recv, nsend, nrecv, local):
    me, cls = lax.axis_index("draw"), lax.axis_index("cls")
    rows = mean.shape[0]
    barrier = pltpu.get_barrier_semaphore()
    for k in range(1, n):
        pl.semaphore_signal(barrier, inc=1, device_id=(cls, lax.rem(me + k, n)), device_id_type=MESH)
    pl.semaphore_wait(barrier, n - 1)

    def noise_copy(slot, k, device):
        return pltpu.make_async_remote_copy(
            noise, noise_out.at[slot], nsend.at[k], nrecv.at[slot], device_id=(cls, device), device_id_type=MESH
        )

    def block_copy(head, owner, k, width, source, device):
        ref = (mean, scale)[head]
        start = pl.multiple_of(owner * tile, 128)
        return pltpu.make_async_remote_copy(
            ref.at[:, pl.ds(start, width)],
            out.at[head, pl.ds(pl.multiple_of(source * rows, rows), rows), pl.ds(0, width)],
            send.at[head, k],
            recv.at[head, source],
            device_id=(cls, device),
            device_id_type=MESH,
        )

    def own_copy(head, width):
        ref = (mean, scale)[head]
        return pltpu.make_async_copy(
            ref.at[:, pl.ds(pl.multiple_of(me * tile, 128), width)],
            out.at[head, pl.ds(pl.multiple_of(me * rows, rows), rows), pl.ds(0, width)],
            local.at[head],
        )

    own_noise = pltpu.make_async_copy(noise, noise_out.at[me], local.at[2])
    for k in range(1, n):
        to = lax.rem(me + k, n)
        for head in range(2):
            at_width(to, full, part, tile, lambda w: block_copy(head, to, k, w, me, to).start())
    for k in range(1, n):
        to = lax.rem(me + k, n)
        noise_copy(me, k, to).start()
    own_noise.start()
    for head in range(2):
        at_width(me, full, part, tile, lambda w: own_copy(head, w).start())
    for k in range(1, n):
        source = lax.rem(me + n - k, n)
        for head in range(2):
            at_width(me, full, part, tile, lambda w: block_copy(head, me, k, w, source, source).wait_recv())
        noise_copy(source, k, source).wait_recv()
    for k in range(1, n):
        to = lax.rem(me + k, n)
        for head in range(2):
            at_width(to, full, part, tile, lambda w: block_copy(head, to, k, w, me, to).wait_send())
        noise_copy(me, k, to).wait_send()
    own_noise.wait()
    for head in range(2):
        at_width(me, full, part, tile, lambda w: own_copy(head, w).wait())


def gather_kernel(n, tile, full, part, cot, out, send, recv, local):
    me, cls = lax.axis_index("draw"), lax.axis_index("cls")
    half = n // 2
    group, side = lax.div(me, 2), lax.rem(me, 2)
    partner = group * 2 + 1 - side
    barrier = pltpu.get_barrier_semaphore()
    peers = [partner] + [lax.rem(group + k, half) * 2 + side for k in range(1, half)]
    for peer in peers:
        pl.semaphore_signal(barrier, inc=1, device_id=(cls, peer), device_id_type=MESH)
    pl.semaphore_wait(barrier, half)

    def place(owner, width):
        return out.at[:, :, pl.ds(pl.multiple_of(owner * tile, 128), width)]

    def from_cot(owner, slot, width, device):
        return pltpu.make_async_remote_copy(
            cot.at[:, :, pl.ds(0, width)], place(owner, width), send.at[slot], recv.at[owner],
            device_id=(cls, device), device_id_type=MESH,
        )

    def forward(owner, slot, width, device):
        return pltpu.make_async_remote_copy(
            place(owner, width), place(owner, width), send.at[slot], recv.at[owner],
            device_id=(cls, device), device_id_type=MESH,
        )

    def own_copy(width):
        return pltpu.make_async_copy(cot.at[:, :, pl.ds(0, width)], place(me, width), local)

    for k in range(1, half):
        at_width(me, full, part, tile, lambda w: from_cot(me, k, w, peers[k]).start())
    at_width(me, full, part, tile, lambda w: from_cot(me, 0, w, partner).start())
    at_width(me, full, part, tile, lambda w: own_copy(w).start())
    order = sorted(range(1, half), key=lambda k: min(k, half - k))
    for k in order:
        owner = peers[k]
        at_width(owner, full, part, tile, lambda w: from_cot(owner, k, w, owner).wait_recv())
        at_width(owner, full, part, tile, lambda w: forward(owner, half + k, w, partner).start())
    at_width(partner, full, part, tile, lambda w: from_cot(partner, 0, w, partner).wait_recv())
    for k in range(1, half):
        owner = lax.rem(group + k, half) * 2 + 1 - side
        at_width(owner, full, part, tile, lambda w: forward(owner, half + k, w, partner).wait_recv())
    for k in range(half):
        at_width(me, full, part, tile, lambda w: from_cot(me, k, w, partner).wait_send())
    for k in range(1, half):
        owner = peers[k]
        at_width(owner, full, part, tile, lambda w: forward(owner, half + k, w, partner).wait_send())
    at_width(me, full, part, tile, lambda w: own_copy(w).wait())


def merge(slots, count, softmax):
    if not softmax:
        total = slots[0]
        for i in range(1, count):
            total = total + slots[i]
        return total
    top = slots[0, 0]
    for i in range(1, count):
        top = jnp.maximum(top, slots[i, 0])
    total = jnp.zeros_like(top)
    for i in range(count):
        total = total + slots[i, 1] * jnp.exp(slots[i, 0] - top)
    return jnp.stack((top, total))


def reduce_kernel(counts, softmax, x, out, *scratch):
    levels = len(counts)
    slots, sends, recvs = scratch[:levels], scratch[levels : 2 * levels], scratch[2 * levels :]
    cls, draw = lax.axis_index("cls"), lax.axis_index("draw")

    def device(level, index):
        return (index, draw) if level == 0 else (cls, index)

    barrier = pltpu.get_barrier_semaphore()
    for level, n in enumerate(counts):
        me = (cls, draw)[level]
        for k in range(1, n):
            pl.semaphore_signal(
                barrier, inc=1, device_id=device(level, lax.rem(me + k, n)), device_id_type=MESH
            )
    pl.semaphore_wait(barrier, sum(counts) - levels)
    value = x[...]
    for level, n in enumerate(counts):
        me = (cls, draw)[level]
        held = slots[level]
        held[me] = value

        def copy(slot, k, target):
            return pltpu.make_async_remote_copy(
                held.at[slot], held.at[slot], sends[level].at[k], recvs[level].at[slot],
                device_id=device(level, target), device_id_type=MESH,
            )

        for k in range(1, n):
            copy(me, k, lax.rem(me + k, n)).start()
        for k in range(1, n):
            source = lax.rem(me + n - k, n)
            copy(source, k, source).wait_recv()
        for k in range(1, n):
            copy(me, k, lax.rem(me + k, n)).wait_send()
        value = merge(held, n, softmax)
    if softmax:
        out[...] = value[0] + jnp.log(value[1])
    else:
        out[...] = value


def params(collective_id):
    return pltpu.CompilerParams(
        collective_id=collective_id, has_side_effects=True, vmem_limit_bytes=32 * 2**20
    )


def reduce_over(x, counts, softmax, collective_id):
    shape = x.shape[1:] if softmax else x.shape
    return pl.pallas_call(
        functools.partial(reduce_kernel, counts, softmax),
        out_shape=jax.ShapeDtypeStruct(shape, jnp.float32),
        in_specs=[VMEM],
        out_specs=VMEM,
        scratch_shapes=[pltpu.VMEM((n,) + x.shape, jnp.float32) for n in counts]
        + [pltpu.SemaphoreType.DMA((n,)) for n in counts]
        + [pltpu.SemaphoreType.DMA((n,)) for n in counts],
        compiler_params=params(collective_id),
    )(x)


def on_device(features, mean_head, scale_head, factor, noise, labels):
    rows, columns = mean_head.shape
    batch = features.shape[0]
    n, ncls = lax.axis_size("draw"), lax.axis_size("cls")
    me = lax.axis_index("draw")
    tiles = -(-columns // 128)
    tile = -(-tiles // n) * 128
    full, part = (tiles * 128) // tile, (tiles * 128) % tile
    padded = n * tile
    own, rank = noise.shape[0], noise.shape[2]
    draws = own * n
    widen = lambda a: jnp.pad(a, ((0, 0), (0, padded - columns)))

    heads, noise_t = pl.pallas_call(
        functools.partial(exchange_kernel, n, tile, full, part),
        out_shape=(
            jax.ShapeDtypeStruct((2, n * rows, tile), jnp.bfloat16),
            jax.ShapeDtypeStruct((n, own, rank, batch), jnp.bfloat16),
        ),
        in_specs=[ANY, ANY, ANY],
        out_specs=(ANY, ANY),
        scratch_shapes=[
            pltpu.SemaphoreType.DMA((2, n)),
            pltpu.SemaphoreType.DMA((2, n)),
            pltpu.SemaphoreType.DMA((n,)),
            pltpu.SemaphoreType.DMA((n,)),
            pltpu.SemaphoreType.DMA((3,)),
        ],
        compiler_params=params(0),
    )(widen(mean_head), widen(scale_head), noise.transpose(0, 2, 1))

    first = me * tile
    local_ids = first + jnp.arange(tile, dtype=jnp.int32)
    valid = local_ids < columns
    class_ids = lax.axis_index("cls") * columns + local_ids
    shift = jnp.where(class_ids >= CREAL, 30000.0, 0.0).astype(jnp.float32)
    my_factor = lax.dynamic_slice_in_dim(jnp.pad(factor, ((0, padded - columns), (0, 0))), first, tile, 0)
    my_labels = lax.dynamic_slice_in_dim(widen(labels), first, tile, 1)

    mean_logit = jnp.dot(features, heads[0], preferred_element_type=jnp.float32)
    scale_pre = jnp.dot(features, heads[1], preferred_element_type=jnp.float32)
    scale_pre = jnp.where(valid[None], scale_pre, 0.0)
    spread = jax.nn.softplus(scale_pre)
    lowrank = lax.dot_general(
        noise_t.reshape(draws, rank, batch), my_factor, (((1,), (1,)), ((), ())), preferred_element_type=jnp.float32
    )
    logits = mean_logit[None] + spread[None] * lowrank - shift[None, None, :]
    logits = jnp.where(valid[None, None, :], logits, -1e30)
    local_top = jnp.max(logits, axis=2)
    local_total = jnp.sum(jnp.exp(logits - local_top[:, :, None]), axis=2)
    lse = reduce_over(jnp.stack((local_top, local_total)), (ncls, n), True, 1)
    log_prob = logits - lse[:, :, None]
    best = jnp.max(log_prob, axis=0)
    mix = best + jnp.log(jnp.sum(jnp.exp(log_prob - best[None]), axis=0))
    ratio = jnp.exp(log_prob - mix[None])
    label_dot = reduce_over(jnp.sum(my_labels[None] * ratio, axis=2), (ncls, n), False, 2)
    logit_cot = (jnp.exp(log_prob) * label_dot[:, :, None] - my_labels[None] * ratio) / batch
    dmean = jnp.sum(logit_cot, axis=0)
    dspread = jnp.sum(logit_cot * lowrank, axis=0)
    cots = jnp.stack((dmean, dspread * jax.nn.sigmoid(scale_pre))).astype(jnp.bfloat16)

    gathered = pl.pallas_call(
        functools.partial(gather_kernel, n, tile, full, part),
        out_shape=jax.ShapeDtypeStruct((2, batch, padded), jnp.bfloat16),
        in_specs=[ANY],
        out_specs=ANY,
        scratch_shapes=[
            pltpu.SemaphoreType.DMA((n,)),
            pltpu.SemaphoreType.DMA((n,)),
            pltpu.SemaphoreType.DMA,
        ],
        compiler_params=params(3),
    )(cots)
    mean_cot, scale_cot = gathered[0, :, :columns], gathered[1, :, :columns]
    my_columns = lax.dynamic_slice_in_dim(features, me * rows, rows, 1)
    contract = (((0,), (0,)), ((), ()))
    across = (((1,), (1,)), ((), ()))
    feature_part = lax.dot_general(
        mean_cot, mean_head, across, preferred_element_type=jnp.float32
    ) + lax.dot_general(scale_cot, scale_head, across, preferred_element_type=jnp.float32)
    mean_grad = lax.dot_general(my_columns, mean_cot, contract, preferred_element_type=jnp.float32)
    scale_grad = lax.dot_general(my_columns, scale_cot, contract, preferred_element_type=jnp.float32)
    feature_grad = reduce_over(feature_part, (ncls,), False, 4)
    return (mean_grad, scale_grad, feature_grad)


def solution(mesh):
    return jax.shard_map(
        on_device,
        mesh=mesh,
        in_specs=(
            P(),
            P("draw", "cls"),
            P("draw", "cls"),
            P("cls", None),
            P("draw", None, None),
            P(None, "cls"),
        ),
        out_specs=(P("draw", "cls"), P("draw", "cls"), P(None, "draw")),
        check_vma=False,
    )
```

```python
import functools
import jax
import jax.numpy as jnp
from jax import lax
from jax.experimental import pallas as pl
from jax.experimental.pallas import tpu as pltpu
from jax.sharding import PartitionSpec as P

CREAL = 21843
UNIT = 16
MESH = pl.DeviceIdType.MESH
ANY = pl.BlockSpec(memory_space=pl.ANY)
VMEM = pl.BlockSpec(memory_space=pltpu.VMEM)


def start_of(owner, n, units):
    return lax.div(owner * units, n)


def at_width(owner, n, units, run):
    base = units // n
    wide = start_of(owner + 1, n, units) - start_of(owner, n, units) > base
    pl.when(wide)(functools.partial(run, (base + 1) * UNIT))
    pl.when(jnp.logical_not(wide))(functools.partial(run, base * UNIT))


def exchange_kernel(n, units, mean, scale, noise, out, noise_out, send, recv, nsend, nrecv, local):
    me, cls = lax.axis_index("draw"), lax.axis_index("cls")
    rows = mean.shape[1]
    barrier = pltpu.get_barrier_semaphore()
    for k in range(1, n):
        pl.semaphore_signal(barrier, inc=1, device_id=(cls, lax.rem(me + k, n)), device_id_type=MESH)
    pl.semaphore_wait(barrier, n - 1)

    def place(head, source, width):
        if rows % 128:
            return out.at[head, source, pl.ds(0, width)]
        return out.at[head, pl.ds(0, width), pl.ds(pl.multiple_of(source * rows, rows), rows)]

    def block(head, owner, width):
        start = pl.multiple_of(start_of(owner, n, units) * UNIT, UNIT)
        return (mean, scale)[head].at[pl.ds(start, width)]

    def remote(source, target, send_sem, recv_sem, device):
        return pltpu.make_async_remote_copy(
            source, target, send_sem, recv_sem, device_id=(cls, device), device_id_type=MESH
        )

    def noise_copy(slot, k, device):
        return remote(noise, noise_out.at[slot], nsend.at[k], nrecv.at[slot], device)

    def each(owner, k, source, device, act):
        for head in range(2):
            at_width(
                owner, n, units,
                lambda w: act(
                    remote(block(head, owner, w), place(head, source, w), send.at[head, k], recv.at[head, source], device)
                ),
            )

    def own(act):
        act(pltpu.make_async_copy(noise, noise_out.at[me], local.at[2]))
        for head in range(2):
            at_width(
                me, n, units,
                lambda w: act(pltpu.make_async_copy(block(head, me, w), place(head, me, w), local.at[head])),
            )

    for k in range(1, n):
        to = lax.rem(me + k, n)
        each(to, k, me, to, lambda c: c.start())
        noise_copy(me, k, to).start()
    own(lambda c: c.start())
    for k in range(1, n):
        source = lax.rem(me + n - k, n)
        each(me, k, source, source, lambda c: c.wait_recv())
        noise_copy(source, k, source).wait_recv()
    for k in range(1, n):
        to = lax.rem(me + k, n)
        each(to, k, me, to, lambda c: c.wait_send())
        noise_copy(me, k, to).wait_send()
    own(lambda c: c.wait())


def gather_kernel(n, units, cot, out, send, recv, local):
    me, cls = lax.axis_index("draw"), lax.axis_index("cls")
    half = n // 2
    group, side = lax.div(me, 2), lax.rem(me, 2)
    partner = group * 2 + 1 - side
    split = units // n // 2 * UNIT
    pieces = [(head, part) for head in range(2) for part in range(2)]
    barrier = pltpu.get_barrier_semaphore()
    peers = [partner] + [lax.rem(group + k, half) * 2 + side for k in range(1, half)]
    for peer in peers:
        pl.semaphore_signal(barrier, inc=1, device_id=(cls, peer), device_id_type=MESH)
    pl.semaphore_wait(barrier, half)

    def source(piece, width):
        head, part = pieces[piece]
        return cot.at[head, pl.ds(split, width - split) if part else pl.ds(0, split)]

    def place(piece, owner, width):
        head, part = pieces[piece]
        start = start_of(owner, n, units) * UNIT + part * split
        return out.at[head, pl.ds(pl.multiple_of(start, UNIT), width - split if part else split)]

    def send_own(piece, owner, slot, device, act):
        at_width(
            owner, n, units,
            lambda w: act(
                pltpu.make_async_remote_copy(
                    source(piece, w), place(piece, owner, w), send.at[slot, piece], recv.at[owner, piece],
                    device_id=(cls, device), device_id_type=MESH,
                )
            ),
        )

    def forward(piece, owner, slot, act):
        at_width(
            owner, n, units,
            lambda w: act(
                pltpu.make_async_remote_copy(
                    place(piece, owner, w), place(piece, owner, w), send.at[slot, piece], recv.at[owner, piece],
                    device_id=(cls, partner), device_id_type=MESH,
                )
            ),
        )

    def own(piece, act):
        at_width(
            me, n, units,
            lambda w: act(pltpu.make_async_copy(source(piece, w), place(piece, me, w), local.at[piece])),
        )

    count = len(pieces)
    for piece in range(count):
        for k in range(1, half):
            send_own(piece, me, k, peers[k], lambda c: c.start())
        send_own(piece, me, 0, partner, lambda c: c.start())
    for piece in range(count):
        own(piece, lambda c: c.start())
    order = sorted(range(1, half), key=lambda k: min(k, half - k))
    for piece in range(count):
        for k in order:
            send_own(piece, peers[k], k, peers[k], lambda c: c.wait_recv())
            forward(piece, peers[k], half + k, lambda c: c.start())
    for piece in range(count):
        send_own(piece, partner, 0, partner, lambda c: c.wait_recv())
        for k in range(1, half):
            owner = lax.rem(group + k, half) * 2 + 1 - side
            forward(piece, owner, half + k, lambda c: c.wait_recv())
    for piece in range(count):
        for k in range(half):
            send_own(piece, me, k, peers[k], lambda c: c.wait_send())
        for k in range(1, half):
            forward(piece, peers[k], half + k, lambda c: c.wait_send())
        own(piece, lambda c: c.wait())


def merge(slots, count, softmax):
    if not softmax:
        total = slots[0]
        for i in range(1, count):
            total = total + slots[i]
        return total
    top = slots[0, 0]
    for i in range(1, count):
        top = jnp.maximum(top, slots[i, 0])
    total = jnp.zeros_like(top)
    for i in range(count):
        total = total + slots[i, 1] * jnp.exp(slots[i, 0] - top)
    return jnp.stack((top, total))


def reduce_kernel(counts, softmax, x, out, *scratch):
    levels = len(counts)
    slots, sends, recvs = scratch[:levels], scratch[levels : 2 * levels], scratch[2 * levels :]
    cls, draw = lax.axis_index("cls"), lax.axis_index("draw")

    def device(level, index):
        return (index, draw) if level == 0 else (cls, index)

    barrier = pltpu.get_barrier_semaphore()
    for level, n in enumerate(counts):
        me = (cls, draw)[level]
        for k in range(1, n):
            pl.semaphore_signal(
                barrier, inc=1, device_id=device(level, lax.rem(me + k, n)), device_id_type=MESH
            )
    pl.semaphore_wait(barrier, sum(counts) - levels)
    value = x[...]
    for level, n in enumerate(counts):
        me = (cls, draw)[level]
        held = slots[level]
        held[me] = value

        def copy(slot, k, target):
            return pltpu.make_async_remote_copy(
                held.at[slot], held.at[slot], sends[level].at[k], recvs[level].at[slot],
                device_id=device(level, target), device_id_type=MESH,
            )

        for k in range(1, n):
            copy(me, k, lax.rem(me + k, n)).start()
        for k in range(1, n):
            source = lax.rem(me + n - k, n)
            copy(source, k, source).wait_recv()
        for k in range(1, n):
            copy(me, k, lax.rem(me + k, n)).wait_send()
        value = merge(held, n, softmax)
    if softmax:
        out[...] = value[0] + jnp.log(value[1])
    else:
        out[...] = value


def params(collective_id):
    return pltpu.CompilerParams(
        collective_id=collective_id, has_side_effects=True, vmem_limit_bytes=32 * 2**20
    )


def reduce_over(x, counts, softmax, collective_id):
    shape = x.shape[1:] if softmax else x.shape
    return pl.pallas_call(
        functools.partial(reduce_kernel, counts, softmax),
        out_shape=jax.ShapeDtypeStruct(shape, jnp.float32),
        in_specs=[VMEM],
        out_specs=VMEM,
        scratch_shapes=[pltpu.VMEM((n,) + x.shape, jnp.float32) for n in counts]
        + [pltpu.SemaphoreType.DMA((n,)) for n in counts]
        + [pltpu.SemaphoreType.DMA((n,)) for n in counts],
        compiler_params=params(collective_id),
    )(x)


def on_device(features, mean_head, scale_head, factor, noise, labels):
    rows, columns = mean_head.shape
    batch = features.shape[0]
    n, ncls = lax.axis_size("draw"), lax.axis_size("cls")
    me = lax.axis_index("draw")
    units = columns // UNIT
    tile = -(-units // n) * UNIT
    own, rank = noise.shape[0], noise.shape[2]
    draws = own * n
    mean_rows, scale_rows = mean_head.T, scale_head.T
    held = (2, tile, n * rows) if rows % 128 == 0 else (2, n, tile, rows)

    heads, noise_t = pl.pallas_call(
        functools.partial(exchange_kernel, n, units),
        out_shape=(
            jax.ShapeDtypeStruct(held, jnp.bfloat16),
            jax.ShapeDtypeStruct((n, own, rank, batch), jnp.bfloat16),
        ),
        in_specs=[ANY] * 3,
        out_specs=(ANY, ANY),
        scratch_shapes=[
            pltpu.SemaphoreType.DMA((2, n)),
            pltpu.SemaphoreType.DMA((2, n)),
            pltpu.SemaphoreType.DMA((n,)),
            pltpu.SemaphoreType.DMA((n,)),
            pltpu.SemaphoreType.DMA((3,)),
        ],
        compiler_params=params(0),
    )(mean_rows, scale_rows, noise.transpose(0, 2, 1))
    if rows % 128:
        heads = heads.transpose(0, 2, 1, 3).reshape(2, tile, n * rows)

    first = start_of(me, n, units) * UNIT
    width = start_of(me + 1, n, units) * UNIT - first
    offsets = jnp.arange(tile, dtype=jnp.int32)[:, None]
    valid = offsets < width
    class_ids = lax.axis_index("cls") * columns + first + offsets
    shift = jnp.where(class_ids >= CREAL, 30000.0, 0.0).astype(jnp.float32)
    my_factor = lax.dynamic_slice_in_dim(factor.T, first, tile, 1)
    my_labels = jnp.where(valid, lax.dynamic_slice_in_dim(labels.T, first, tile, 0), 0.0)

    last_dims = (((1,), (1,)), ((), ()))
    mean_logit = lax.dot_general(heads[0], features, last_dims, preferred_element_type=jnp.float32)
    scale_pre = lax.dot_general(heads[1], features, last_dims, preferred_element_type=jnp.float32)
    scale_pre = jnp.where(valid, scale_pre, 0.0)
    spread = jax.nn.softplus(scale_pre)
    lowrank = jnp.einsum(
        "rc,srb->scb", my_factor, noise_t.reshape(draws, rank, batch), preferred_element_type=jnp.float32
    )
    logits = mean_logit[None] + spread[None] * lowrank - shift[None]
    logits = jnp.where(valid[None], logits, -1e30)
    local_top = jnp.max(logits, axis=1)
    local_total = jnp.sum(jnp.exp(logits - local_top[:, None]), axis=1)
    lse = reduce_over(jnp.stack((local_top, local_total)), (ncls, n), True, 1)
    log_prob = logits - lse[:, None]
    best = jnp.max(log_prob, axis=0)
    mix = best + jnp.log(jnp.sum(jnp.exp(log_prob - best[None]), axis=0))
    ratio = jnp.exp(log_prob - mix[None])
    label_dot = reduce_over(jnp.sum(my_labels[None] * ratio, axis=1), (ncls, n), False, 2)
    logit_cot = (jnp.exp(log_prob) * label_dot[:, None] - my_labels[None] * ratio) / batch
    dmean = jnp.sum(logit_cot, axis=0)
    dspread = jnp.sum(logit_cot * lowrank, axis=0)
    cots = jnp.stack((dmean, dspread * jax.nn.sigmoid(scale_pre))).astype(jnp.bfloat16)

    gathered = pl.pallas_call(
        functools.partial(gather_kernel, n, units),
        out_shape=jax.ShapeDtypeStruct((2, columns, batch), jnp.bfloat16),
        in_specs=[ANY],
        out_specs=ANY,
        scratch_shapes=[
            pltpu.SemaphoreType.DMA((n, 4)),
            pltpu.SemaphoreType.DMA((n, 4)),
            pltpu.SemaphoreType.DMA((4,)),
        ],
        compiler_params=params(3),
    )(cots)
    mean_cot, scale_cot = gathered[0], gathered[1]
    my_columns = lax.dynamic_slice_in_dim(features, me * rows, rows, 1)
    over_classes = (((0,), (0,)), ((), ()))
    feature_part = lax.dot_general(
        mean_cot, mean_rows, over_classes, preferred_element_type=jnp.float32
    ) + lax.dot_general(scale_cot, scale_rows, over_classes, preferred_element_type=jnp.float32)
    mean_grad = jnp.dot(mean_cot, my_columns, preferred_element_type=jnp.float32).T
    scale_grad = jnp.dot(scale_cot, my_columns, preferred_element_type=jnp.float32).T
    feature_grad, step = feature_part, 1
    while step < ncls:
        feature_grad = feature_grad + lax.ppermute(feature_grad, "cls", [(i, i ^ step) for i in range(ncls)])
        step *= 2
    return (mean_grad, scale_grad, feature_grad)


def solution(mesh):
    return jax.shard_map(
        on_device,
        mesh=mesh,
        in_specs=(
            P(),
            P("draw", "cls"),
            P("draw", "cls"),
            P("cls", None),
            P("draw", None, None),
            P(None, "cls"),
        ),
        out_specs=(P("draw", "cls"), P("draw", "cls"), P(None, "draw")),
        check_vma=False,
    )
```

```python
import functools
import jax
import jax.numpy as jnp
from jax import lax
from jax.experimental import pallas as pl
from jax.experimental.pallas import tpu as pltpu
from jax.sharding import PartitionSpec as P

CREAL = 21843
UNIT = 16
MESH = pl.DeviceIdType.MESH
ANY = pl.BlockSpec(memory_space=pl.ANY)
VMEM = pl.BlockSpec(memory_space=pltpu.VMEM)


def start_of(owner, n, units):
    return lax.div(owner * units, n)


def at_width(owner, n, units, run):
    base = units // n
    wide = start_of(owner + 1, n, units) - start_of(owner, n, units) > base
    pl.when(wide)(functools.partial(run, (base + 1) * UNIT))
    pl.when(jnp.logical_not(wide))(functools.partial(run, base * UNIT))


def exchange_kernel(
    n, units, feat, mean, scale, noise, logits, noise_out, held, part_out, part_in,
    send, recv, part_send, part_recv, nsend, nrecv, local, nlocal,
):
    me, cls = lax.axis_index("draw"), lax.axis_index("cls")
    half = n // 2
    mirror = lax.rem(me + half, n)
    base, spot = lax.div(me, half) * half, lax.rem(me, half)
    barrier = pltpu.get_barrier_semaphore()
    for k in range(1, n):
        pl.semaphore_signal(barrier, inc=1, device_id=(cls, lax.rem(me + k, n)), device_id_type=MESH)
    pl.semaphore_wait(barrier, n - 1)

    def remote(source, target, send_sem, recv_sem, device):
        return pltpu.make_async_remote_copy(
            source, target, send_sem, recv_sem, device_id=(cls, device), device_id_type=MESH
        )

    def noise_copy(slot, k, device):
        return remote(noise, noise_out.at[slot], nsend.at[k], nrecv.at[slot], device)

    def block(head, owner, width):
        start = pl.multiple_of(start_of(owner, n, units) * UNIT, UNIT)
        return (mean, scale)[head].at[pl.ds(start, width)]

    def block_copy(far, head, owner, k, source, device, act):
        at_width(
            owner, n, units,
            lambda w: act(
                remote(
                    block(head, owner, w), held.at[far, head, source, pl.ds(0, w)],
                    send.at[far, head, k], recv.at[far, head, source], device,
                )
            ),
        )

    def own_copy(far, head, act):
        owner = mirror if far else me
        at_width(
            owner, n, units,
            lambda w: act(
                pltpu.make_async_copy(
                    block(head, owner, w), held.at[far, head, spot, pl.ds(0, w)], local.at[far, head]
                )
            ),
        )

    def sends(far, head, act):
        for k in range(1, half):
            peer = base + lax.rem(spot + k, half)
            block_copy(far, head, lax.rem(peer + half, n) if far else peer, k, spot, peer, act)

    def arrive(far, head):
        owner = mirror if far else me
        for k in range(1, half):
            source = lax.rem(spot + half - k, half)
            block_copy(far, head, owner, k, source, base + source, lambda c: c.wait_recv())
        own_copy(far, head, lambda c: c.wait())
        total = None
        for source in range(half):
            term = lax.dot_general(
                held[far, head, source], feat[source], (((1,), (1,)), ((), ())), preferred_element_type=jnp.float32
            )
            total = term if total is None else total + term
        return total

    def part_copy(head):
        return remote(part_out.at[head], part_in.at[head], part_send.at[head], part_recv.at[head], mirror)

    own_noise = pltpu.make_async_copy(noise, noise_out.at[me], nlocal)
    stages = [(1, 0), (1, 1), (0, 0), (0, 1)]
    sends(1, 0, lambda c: c.start())
    for k in range(1, n):
        noise_copy(me, k, lax.rem(me + k, n)).start()
    for far, head in stages[1:]:
        sends(far, head, lambda c: c.start())
    for far, head in stages:
        own_copy(far, head, lambda c: c.start())
    own_noise.start()
    for head in range(2):
        part_out[head] = arrive(1, head)
        part_copy(head).start()
    for head in range(2):
        logits[head] = arrive(0, head)
    for k in range(1, n):
        source = lax.rem(me + n - k, n)
        noise_copy(source, k, source).wait_recv()
    own_noise.wait()
    for head in range(2):
        part_copy(head).wait_recv()
        logits[head] = logits[head] + part_in[head]
    for far, head in stages:
        sends(far, head, lambda c: c.wait_send())
    for k in range(1, n):
        noise_copy(me, k, lax.rem(me + k, n)).wait_send()
    for head in range(2):
        part_copy(head).wait_send()


def gather_kernel(n, units, cot, out, send, recv, local):
    me, cls = lax.axis_index("draw"), lax.axis_index("cls")
    half = n // 2
    group, side = lax.div(me, 2), lax.rem(me, 2)
    partner = group * 2 + 1 - side
    split = units // n // 2 * UNIT
    pieces = [(head, part) for head in range(2) for part in range(2)]
    barrier = pltpu.get_barrier_semaphore()
    peers = [partner] + [lax.rem(group + k, half) * 2 + side for k in range(1, half)]
    for peer in peers:
        pl.semaphore_signal(barrier, inc=1, device_id=(cls, peer), device_id_type=MESH)
    pl.semaphore_wait(barrier, half)

    def source(piece, width):
        head, part = pieces[piece]
        return cot.at[head, pl.ds(split, width - split) if part else pl.ds(0, split)]

    def place(piece, owner, width):
        head, part = pieces[piece]
        start = start_of(owner, n, units) * UNIT + part * split
        return out.at[head, pl.ds(pl.multiple_of(start, UNIT), width - split if part else split)]

    def send_own(piece, owner, slot, device, act):
        at_width(
            owner, n, units,
            lambda w: act(
                pltpu.make_async_remote_copy(
                    source(piece, w), place(piece, owner, w), send.at[slot, piece], recv.at[owner, piece],
                    device_id=(cls, device), device_id_type=MESH,
                )
            ),
        )

    def forward(piece, owner, slot, act):
        at_width(
            owner, n, units,
            lambda w: act(
                pltpu.make_async_remote_copy(
                    place(piece, owner, w), place(piece, owner, w), send.at[slot, piece], recv.at[owner, piece],
                    device_id=(cls, partner), device_id_type=MESH,
                )
            ),
        )

    def own(piece, act):
        at_width(
            me, n, units,
            lambda w: act(pltpu.make_async_copy(source(piece, w), place(piece, me, w), local.at[piece])),
        )

    count = len(pieces)
    for piece in range(count):
        for k in range(1, half):
            send_own(piece, me, k, peers[k], lambda c: c.start())
        send_own(piece, me, 0, partner, lambda c: c.start())
    for piece in range(count):
        own(piece, lambda c: c.start())
    order = sorted(range(1, half), key=lambda k: min(k, half - k))
    for piece in range(count):
        for k in order:
            send_own(piece, peers[k], k, peers[k], lambda c: c.wait_recv())
            forward(piece, peers[k], half + k, lambda c: c.start())
    for piece in range(count):
        send_own(piece, partner, 0, partner, lambda c: c.wait_recv())
        for k in range(1, half):
            owner = lax.rem(group + k, half) * 2 + 1 - side
            forward(piece, owner, half + k, lambda c: c.wait_recv())
    for piece in range(count):
        for k in range(half):
            send_own(piece, me, k, peers[k], lambda c: c.wait_send())
        for k in range(1, half):
            forward(piece, peers[k], half + k, lambda c: c.wait_send())
        own(piece, lambda c: c.wait())


def merge(slots, count, softmax):
    if not softmax:
        total = slots[0]
        for i in range(1, count):
            total = total + slots[i]
        return total
    top = slots[0, 0]
    for i in range(1, count):
        top = jnp.maximum(top, slots[i, 0])
    total = jnp.zeros_like(top)
    for i in range(count):
        total = total + slots[i, 1] * jnp.exp(slots[i, 0] - top)
    return jnp.stack((top, total))


def reduce_kernel(counts, softmax, x, out, *scratch):
    levels = len(counts)
    slots, sends, recvs = scratch[:levels], scratch[levels : 2 * levels], scratch[2 * levels :]
    cls, draw = lax.axis_index("cls"), lax.axis_index("draw")

    def device(level, index):
        return (index, draw) if level == 0 else (cls, index)

    barrier = pltpu.get_barrier_semaphore()
    for level, n in enumerate(counts):
        me = (cls, draw)[level]
        for k in range(1, n):
            pl.semaphore_signal(
                barrier, inc=1, device_id=device(level, lax.rem(me + k, n)), device_id_type=MESH
            )
    pl.semaphore_wait(barrier, sum(counts) - levels)
    value = x[...]
    for level, n in enumerate(counts):
        me = (cls, draw)[level]
        held = slots[level]
        held[me] = value

        def copy(slot, k, target):
            return pltpu.make_async_remote_copy(
                held.at[slot], held.at[slot], sends[level].at[k], recvs[level].at[slot],
                device_id=device(level, target), device_id_type=MESH,
            )

        for k in range(1, n):
            copy(me, k, lax.rem(me + k, n)).start()
        for k in range(1, n):
            source = lax.rem(me + n - k, n)
            copy(source, k, source).wait_recv()
        for k in range(1, n):
            copy(me, k, lax.rem(me + k, n)).wait_send()
        value = merge(held, n, softmax)
    if softmax:
        out[...] = value[0] + jnp.log(value[1])
    else:
        out[...] = value


def params(collective_id):
    return pltpu.CompilerParams(
        collective_id=collective_id, has_side_effects=True, vmem_limit_bytes=32 * 2**20
    )


def reduce_over(x, counts, softmax, collective_id):
    shape = x.shape[1:] if softmax else x.shape
    return pl.pallas_call(
        functools.partial(reduce_kernel, counts, softmax),
        out_shape=jax.ShapeDtypeStruct(shape, jnp.float32),
        in_specs=[VMEM],
        out_specs=VMEM,
        scratch_shapes=[pltpu.VMEM((n,) + x.shape, jnp.float32) for n in counts]
        + [pltpu.SemaphoreType.DMA((n,)) for n in counts]
        + [pltpu.SemaphoreType.DMA((n,)) for n in counts],
        compiler_params=params(collective_id),
    )(x)


def on_device(features, mean_head, scale_head, factor, noise, labels):
    rows, columns = mean_head.shape
    batch = features.shape[0]
    n, ncls = lax.axis_size("draw"), lax.axis_size("cls")
    me = lax.axis_index("draw")
    units = columns // UNIT
    tile = -(-units // n) * UNIT
    own, rank = noise.shape[0], noise.shape[2]
    draws = own * n
    mean_rows, scale_rows = mean_head.T, scale_head.T
    half = n // 2
    my_half = lax.dynamic_slice_in_dim(features, lax.div(me, half) * (half * rows), half * rows, 1)
    feat = my_half.reshape(batch, half, rows).transpose(1, 0, 2)

    heads, noise_t = pl.pallas_call(
        functools.partial(exchange_kernel, n, units),
        out_shape=(
            jax.ShapeDtypeStruct((2, tile, batch), jnp.float32),
            jax.ShapeDtypeStruct((n, own, rank, batch), jnp.bfloat16),
        ),
        in_specs=[VMEM] + [ANY] * 3,
        out_specs=(VMEM, ANY),
        scratch_shapes=[
            pltpu.VMEM((2, 2, half, tile, rows), jnp.bfloat16),
            pltpu.VMEM((2, tile, batch), jnp.float32),
            pltpu.VMEM((2, tile, batch), jnp.float32),
            pltpu.SemaphoreType.DMA((2, 2, half)),
            pltpu.SemaphoreType.DMA((2, 2, half)),
            pltpu.SemaphoreType.DMA((2,)),
            pltpu.SemaphoreType.DMA((2,)),
            pltpu.SemaphoreType.DMA((n,)),
            pltpu.SemaphoreType.DMA((n,)),
            pltpu.SemaphoreType.DMA((2, 2)),
            pltpu.SemaphoreType.DMA,
        ],
        compiler_params=params(0),
    )(feat, mean_rows, scale_rows, noise.transpose(0, 2, 1))

    first = start_of(me, n, units) * UNIT
    width = start_of(me + 1, n, units) * UNIT - first
    offsets = jnp.arange(tile, dtype=jnp.int32)[:, None]
    valid = offsets < width
    class_ids = lax.axis_index("cls") * columns + first + offsets
    shift = jnp.where(class_ids >= CREAL, 30000.0, 0.0).astype(jnp.float32)
    my_factor = lax.dynamic_slice_in_dim(factor.T, first, tile, 1)
    my_labels = jnp.where(valid, lax.dynamic_slice_in_dim(labels.T, first, tile, 0), 0.0)

    mean_logit, scale_pre = heads[0], heads[1]
    scale_pre = jnp.where(valid, scale_pre, 0.0)
    spread = jax.nn.softplus(scale_pre)
    lowrank = jnp.einsum(
        "rc,srb->scb", my_factor, noise_t.reshape(draws, rank, batch), preferred_element_type=jnp.float32
    )
    logits = mean_logit[None] + spread[None] * lowrank - shift[None]
    logits = jnp.where(valid[None], logits, -1e30)
    local_top = jnp.max(logits, axis=1)
    local_total = jnp.sum(jnp.exp(logits - local_top[:, None]), axis=1)
    lse = reduce_over(jnp.stack((local_top, local_total)), (ncls, n), True, 1)
    log_prob = logits - lse[:, None]
    best = jnp.max(log_prob, axis=0)
    mix = best + jnp.log(jnp.sum(jnp.exp(log_prob - best[None]), axis=0))
    ratio = jnp.exp(log_prob - mix[None])
    label_dot = reduce_over(jnp.sum(my_labels[None] * ratio, axis=1), (ncls, n), False, 2)
    logit_cot = (jnp.exp(log_prob) * label_dot[:, None] - my_labels[None] * ratio) / batch
    dmean = jnp.sum(logit_cot, axis=0)
    dspread = jnp.sum(logit_cot * lowrank, axis=0)
    cots = jnp.stack((dmean, dspread * jax.nn.sigmoid(scale_pre))).astype(jnp.bfloat16)

    gathered = pl.pallas_call(
        functools.partial(gather_kernel, n, units),
        out_shape=jax.ShapeDtypeStruct((2, columns, batch), jnp.bfloat16),
        in_specs=[ANY],
        out_specs=ANY,
        scratch_shapes=[
            pltpu.SemaphoreType.DMA((n, 4)),
            pltpu.SemaphoreType.DMA((n, 4)),
            pltpu.SemaphoreType.DMA((4,)),
        ],
        compiler_params=params(3),
    )(cots)
    mean_cot, scale_cot = gathered[0], gathered[1]
    my_columns = lax.dynamic_slice_in_dim(features, me * rows, rows, 1)
    over_classes = (((0,), (0,)), ((), ()))
    feature_part = lax.dot_general(
        mean_cot, mean_rows, over_classes, preferred_element_type=jnp.float32
    ) + lax.dot_general(scale_cot, scale_rows, over_classes, preferred_element_type=jnp.float32)
    mean_grad = jnp.dot(mean_cot, my_columns, preferred_element_type=jnp.float32).T
    scale_grad = jnp.dot(scale_cot, my_columns, preferred_element_type=jnp.float32).T
    feature_grad, step = feature_part, 1
    while step < ncls:
        feature_grad = feature_grad + lax.ppermute(feature_grad, "cls", [(i, i ^ step) for i in range(ncls)])
        step *= 2
    return (mean_grad, scale_grad, feature_grad)


def solution(mesh):
    return jax.shard_map(
        on_device,
        mesh=mesh,
        in_specs=(
            P(),
            P("draw", "cls"),
            P("draw", "cls"),
            P("cls", None),
            P("draw", None, None),
            P(None, "cls"),
        ),
        out_specs=(P("draw", "cls"), P("draw", "cls"), P(None, "draw")),
        check_vma=False,
    )
```

```python
import functools
import jax
import jax.numpy as jnp
from jax import lax
from jax.experimental import pallas as pl
from jax.experimental.pallas import tpu as pltpu
from jax.sharding import PartitionSpec as P

CREAL = 21843
UNIT = 16
MESH = pl.DeviceIdType.MESH
ANY = pl.BlockSpec(memory_space=pl.ANY)
VMEM = pl.BlockSpec(memory_space=pltpu.VMEM)


def start_of(owner, n, units):
    return lax.div(owner * units, n)


def at_width(owner, n, units, run):
    base = units // n
    wide = start_of(owner + 1, n, units) - start_of(owner, n, units) > base
    pl.when(wide)(functools.partial(run, (base + 1) * UNIT))
    pl.when(jnp.logical_not(wide))(functools.partial(run, base * UNIT))


def exchange_kernel(
    n, units, feat, mean, scale, noise, logits, noise_out, held, part_out, part_in,
    send, recv, part_send, part_recv, nsend, nrecv, local, nlocal,
):
    me, cls = lax.axis_index("draw"), lax.axis_index("cls")
    half, rows = n // 2, mean.shape[1]
    mirror = lax.rem(me + half, n)
    base, spot = lax.div(me, half) * half, lax.rem(me, half)
    barrier = pltpu.get_barrier_semaphore()
    for k in range(1, n):
        pl.semaphore_signal(barrier, inc=1, device_id=(cls, lax.rem(me + k, n)), device_id_type=MESH)
    pl.semaphore_wait(barrier, n - 1)

    def remote(source, target, send_sem, recv_sem, device):
        return pltpu.make_async_remote_copy(
            source, target, send_sem, recv_sem, device_id=(cls, device), device_id_type=MESH
        )

    def noise_copy(slot, k, device):
        return remote(noise, noise_out.at[slot], nsend.at[k], nrecv.at[slot], device)

    def block(head, owner, width):
        start = pl.multiple_of(start_of(owner, n, units) * UNIT, UNIT)
        return (mean, scale)[head].at[pl.ds(start, width)]

    def block_copy(far, head, owner, k, source, device, act):
        at_width(
            owner, n, units,
            lambda w: act(
                remote(
                    block(head, owner, w), held.at[far, head, source, pl.ds(0, w)],
                    send.at[far, head, k], recv.at[far, head, source], device,
                )
            ),
        )

    def own_copy(far, head, act):
        owner = mirror if far else me
        at_width(
            owner, n, units,
            lambda w: act(
                pltpu.make_async_copy(
                    block(head, owner, w), held.at[far, head, spot, pl.ds(0, w)], local.at[far, head]
                )
            ),
        )

    def sends(far, head, act):
        for k in range(1, half):
            peer = base + lax.rem(spot + k, half)
            block_copy(far, head, lax.rem(peer + half, n) if far else peer, k, spot, peer, act)

    def columns_of(source):
        if rows % 128:
            return feat[source]
        return feat[:, pl.ds(pl.multiple_of(source * rows, rows), rows)]

    def arrive(far, head):
        owner = mirror if far else me
        for k in range(1, half):
            source = lax.rem(spot + half - k, half)
            block_copy(far, head, owner, k, source, base + source, lambda c: c.wait_recv())
        own_copy(far, head, lambda c: c.wait())
        total = None
        for source in range(half):
            term = lax.dot_general(
                held[far, head, source], columns_of(base + source), (((1,), (1,)), ((), ())),
                preferred_element_type=jnp.float32,
            )
            total = term if total is None else total + term
        return total

    def part_copy(head):
        return remote(part_out.at[head], part_in.at[head], part_send.at[head], part_recv.at[head], mirror)

    own_noise = pltpu.make_async_copy(noise, noise_out.at[me], nlocal)
    stages = [(1, 0), (1, 1), (0, 0), (0, 1)]
    sends(1, 0, lambda c: c.start())
    for k in range(1, n):
        noise_copy(me, k, lax.rem(me + k, n)).start()
    for far, head in stages[1:]:
        sends(far, head, lambda c: c.start())
    for far, head in stages:
        own_copy(far, head, lambda c: c.start())
    own_noise.start()
    for head in range(2):
        part_out[head] = arrive(1, head)
        part_copy(head).start()
    for head in range(2):
        logits[head] = arrive(0, head)
    for k in range(1, n):
        source = lax.rem(me + n - k, n)
        noise_copy(source, k, source).wait_recv()
    own_noise.wait()
    for head in range(2):
        part_copy(head).wait_recv()
        logits[head] = logits[head] + part_in[head]
    for far, head in stages:
        sends(far, head, lambda c: c.wait_send())
    for k in range(1, n):
        noise_copy(me, k, lax.rem(me + k, n)).wait_send()
    for head in range(2):
        part_copy(head).wait_send()


def gather_kernel(n, units, cot, out, send, recv, local):
    me, cls = lax.axis_index("draw"), lax.axis_index("cls")
    half = n // 2
    group, side = lax.div(me, 2), lax.rem(me, 2)
    partner = group * 2 + 1 - side
    split = units // n // 2 * UNIT
    pieces = [(head, part) for head in range(2) for part in range(2)]
    barrier = pltpu.get_barrier_semaphore()
    peers = [partner] + [lax.rem(group + k, half) * 2 + side for k in range(1, half)]
    for peer in peers:
        pl.semaphore_signal(barrier, inc=1, device_id=(cls, peer), device_id_type=MESH)
    pl.semaphore_wait(barrier, half)

    def source(piece, width):
        head, part = pieces[piece]
        return cot.at[head, pl.ds(split, width - split) if part else pl.ds(0, split)]

    def place(piece, owner, width):
        head, part = pieces[piece]
        start = start_of(owner, n, units) * UNIT + part * split
        return out.at[head, pl.ds(pl.multiple_of(start, UNIT), width - split if part else split)]

    def send_own(piece, owner, slot, device, act):
        at_width(
            owner, n, units,
            lambda w: act(
                pltpu.make_async_remote_copy(
                    source(piece, w), place(piece, owner, w), send.at[slot, piece], recv.at[owner, piece],
                    device_id=(cls, device), device_id_type=MESH,
                )
            ),
        )

    def forward(piece, owner, slot, act):
        at_width(
            owner, n, units,
            lambda w: act(
                pltpu.make_async_remote_copy(
                    place(piece, owner, w), place(piece, owner, w), send.at[slot, piece], recv.at[owner, piece],
                    device_id=(cls, partner), device_id_type=MESH,
                )
            ),
        )

    def own(piece, act):
        at_width(
            me, n, units,
            lambda w: act(pltpu.make_async_copy(source(piece, w), place(piece, me, w), local.at[piece])),
        )

    count = len(pieces)
    for piece in range(count):
        for k in range(1, half):
            send_own(piece, me, k, peers[k], lambda c: c.start())
        send_own(piece, me, 0, partner, lambda c: c.start())
    for piece in range(count):
        own(piece, lambda c: c.start())
    order = sorted(range(1, half), key=lambda k: min(k, half - k))
    for piece in range(count):
        for k in order:
            send_own(piece, peers[k], k, peers[k], lambda c: c.wait_recv())
            forward(piece, peers[k], half + k, lambda c: c.start())
    for piece in range(count):
        send_own(piece, partner, 0, partner, lambda c: c.wait_recv())
        for k in range(1, half):
            owner = lax.rem(group + k, half) * 2 + 1 - side
            forward(piece, owner, half + k, lambda c: c.wait_recv())
    for piece in range(count):
        for k in range(half):
            send_own(piece, me, k, peers[k], lambda c: c.wait_send())
        for k in range(1, half):
            forward(piece, peers[k], half + k, lambda c: c.wait_send())
        own(piece, lambda c: c.wait())


def merge(slots, count, softmax):
    if not softmax:
        total = slots[0]
        for i in range(1, count):
            total = total + slots[i]
        return total
    top = slots[0, 0]
    for i in range(1, count):
        top = jnp.maximum(top, slots[i, 0])
    total = jnp.zeros_like(top)
    for i in range(count):
        total = total + slots[i, 1] * jnp.exp(slots[i, 0] - top)
    return jnp.stack((top, total))


def reduce_kernel(counts, softmax, x, out, *scratch):
    levels = len(counts)
    slots, sends, recvs = scratch[:levels], scratch[levels : 2 * levels], scratch[2 * levels :]
    cls, draw = lax.axis_index("cls"), lax.axis_index("draw")

    def device(level, index):
        return (index, draw) if level == 0 else (cls, index)

    barrier = pltpu.get_barrier_semaphore()
    for level, n in enumerate(counts):
        me = (cls, draw)[level]
        for k in range(1, n):
            pl.semaphore_signal(
                barrier, inc=1, device_id=device(level, lax.rem(me + k, n)), device_id_type=MESH
            )
    pl.semaphore_wait(barrier, sum(counts) - levels)
    value = x[...]
    for level, n in enumerate(counts):
        me = (cls, draw)[level]
        held = slots[level]
        held[me] = value

        def copy(slot, k, target):
            return pltpu.make_async_remote_copy(
                held.at[slot], held.at[slot], sends[level].at[k], recvs[level].at[slot],
                device_id=device(level, target), device_id_type=MESH,
            )

        for k in range(1, n):
            copy(me, k, lax.rem(me + k, n)).start()
        for k in range(1, n):
            source = lax.rem(me + n - k, n)
            copy(source, k, source).wait_recv()
        for k in range(1, n):
            copy(me, k, lax.rem(me + k, n)).wait_send()
        value = merge(held, n, softmax)
    if softmax:
        out[...] = value[0] + jnp.log(value[1])
    else:
        out[...] = value


def params(collective_id, grant=32):
    return pltpu.CompilerParams(
        collective_id=collective_id, has_side_effects=True, vmem_limit_bytes=grant * 2**20
    )


def reduce_over(x, counts, softmax, collective_id):
    shape = x.shape[1:] if softmax else x.shape
    return pl.pallas_call(
        functools.partial(reduce_kernel, counts, softmax),
        out_shape=jax.ShapeDtypeStruct(shape, jnp.float32),
        in_specs=[VMEM],
        out_specs=VMEM,
        scratch_shapes=[pltpu.VMEM((n,) + x.shape, jnp.float32) for n in counts]
        + [pltpu.SemaphoreType.DMA((n,)) for n in counts]
        + [pltpu.SemaphoreType.DMA((n,)) for n in counts],
        compiler_params=params(collective_id),
    )(x)


def on_device(features, mean_head, scale_head, factor, noise, labels):
    rows, columns = mean_head.shape
    batch = features.shape[0]
    n, ncls = lax.axis_size("draw"), lax.axis_size("cls")
    me = lax.axis_index("draw")
    units = columns // UNIT
    tile = -(-units // n) * UNIT
    own, rank = noise.shape[0], noise.shape[2]
    draws = own * n
    mean_rows, scale_rows = mean_head.T, scale_head.T
    half = n // 2
    feat = features.reshape(batch, n, rows).transpose(1, 0, 2) if rows % 128 else features

    heads, noise_t = pl.pallas_call(
        functools.partial(exchange_kernel, n, units),
        out_shape=(
            jax.ShapeDtypeStruct((2, tile, batch), jnp.float32),
            jax.ShapeDtypeStruct((n, own, rank, batch), jnp.bfloat16),
        ),
        in_specs=[VMEM] + [ANY] * 3,
        out_specs=(VMEM, ANY),
        scratch_shapes=[
            pltpu.VMEM((2, 2, half, tile, rows), jnp.bfloat16),
            pltpu.VMEM((2, tile, batch), jnp.float32),
            pltpu.VMEM((2, tile, batch), jnp.float32),
            pltpu.SemaphoreType.DMA((2, 2, half)),
            pltpu.SemaphoreType.DMA((2, 2, half)),
            pltpu.SemaphoreType.DMA((2,)),
            pltpu.SemaphoreType.DMA((2,)),
            pltpu.SemaphoreType.DMA((n,)),
            pltpu.SemaphoreType.DMA((n,)),
            pltpu.SemaphoreType.DMA((2, 2)),
            pltpu.SemaphoreType.DMA,
        ],
        compiler_params=params(0, 60),
    )(feat, mean_rows, scale_rows, noise.transpose(0, 2, 1))

    first = start_of(me, n, units) * UNIT
    width = start_of(me + 1, n, units) * UNIT - first
    offsets = jnp.arange(tile, dtype=jnp.int32)[:, None]
    valid = offsets < width
    class_ids = lax.axis_index("cls") * columns + first + offsets
    shift = jnp.where(class_ids >= CREAL, 30000.0, 0.0).astype(jnp.float32)
    my_factor = lax.dynamic_slice_in_dim(factor.T, first, tile, 1)
    my_labels = jnp.where(valid, lax.dynamic_slice_in_dim(labels.T, first, tile, 0), 0.0)

    mean_logit, scale_pre = heads[0], heads[1]
    scale_pre = jnp.where(valid, scale_pre, 0.0)
    spread = jax.nn.softplus(scale_pre)
    lowrank = jnp.einsum(
        "rc,srb->scb", my_factor, noise_t.reshape(draws, rank, batch), preferred_element_type=jnp.float32
    )
    logits = mean_logit[None] + spread[None] * lowrank - shift[None]
    logits = jnp.where(valid[None], logits, -1e30)
    local_top = jnp.max(logits, axis=1)
    local_total = jnp.sum(jnp.exp(logits - local_top[:, None]), axis=1)
    lse = reduce_over(jnp.stack((local_top, local_total)), (ncls, n), True, 1)
    log_prob = logits - lse[:, None]
    best = jnp.max(log_prob, axis=0)
    risen = jnp.exp(log_prob - best[None])
    inverse = 1.0 / jnp.sum(risen, axis=0)
    weight = my_labels * inverse
    label_dot = reduce_over(jnp.sum(weight[None] * risen, axis=1), (ncls, n), False, 2)
    logit_cot = risen * ((jnp.exp(best) / batch)[None] * label_dot[:, None] - (weight / batch)[None])
    dmean = jnp.sum(logit_cot, axis=0)
    dspread = jnp.sum(logit_cot * lowrank, axis=0)
    cots = jnp.stack((dmean, dspread * jax.nn.sigmoid(scale_pre))).astype(jnp.bfloat16)

    gathered = pl.pallas_call(
        functools.partial(gather_kernel, n, units),
        out_shape=jax.ShapeDtypeStruct((2, columns, batch), jnp.bfloat16),
        in_specs=[ANY],
        out_specs=ANY,
        scratch_shapes=[
            pltpu.SemaphoreType.DMA((n, 4)),
            pltpu.SemaphoreType.DMA((n, 4)),
            pltpu.SemaphoreType.DMA((4,)),
        ],
        compiler_params=params(3),
    )(cots)
    mean_cot, scale_cot = gathered[0], gathered[1]
    my_columns = lax.dynamic_slice_in_dim(features, me * rows, rows, 1)
    over_classes = (((0,), (0,)), ((), ()))
    feature_part = lax.dot_general(
        mean_cot, mean_rows, over_classes, preferred_element_type=jnp.float32
    ) + lax.dot_general(scale_cot, scale_rows, over_classes, preferred_element_type=jnp.float32)
    mean_grad = jnp.dot(mean_cot, my_columns, preferred_element_type=jnp.float32).T
    scale_grad = jnp.dot(scale_cot, my_columns, preferred_element_type=jnp.float32).T
    feature_grad, step = feature_part, 1
    while step < ncls:
        feature_grad = feature_grad + lax.ppermute(feature_grad, "cls", [(i, i ^ step) for i in range(ncls)])
        step *= 2
    return (mean_grad, scale_grad, feature_grad)


def solution(mesh):
    return jax.shard_map(
        on_device,
        mesh=mesh,
        in_specs=(
            P(),
            P("draw", "cls"),
            P("draw", "cls"),
            P("cls", None),
            P("draw", None, None),
            P(None, "cls"),
        ),
        out_specs=(P("draw", "cls"), P("draw", "cls"), P(None, "draw")),
        check_vma=False,
    )
```

```python
import functools
import jax
import jax.numpy as jnp
from jax import lax
from jax.experimental import pallas as pl
from jax.experimental.pallas import tpu as pltpu
from jax.sharding import PartitionSpec as P

CREAL = 21843
UNIT = 16
MESH = pl.DeviceIdType.MESH
ANY = pl.BlockSpec(memory_space=pl.ANY)
VMEM = pl.BlockSpec(memory_space=pltpu.VMEM)


def start_of(owner, n, units):
    return lax.div(owner * units, n)


def at_width(owner, n, units, run):
    base = units // n
    wide = start_of(owner + 1, n, units) - start_of(owner, n, units) > base
    pl.when(wide)(functools.partial(run, (base + 1) * UNIT))
    pl.when(jnp.logical_not(wide))(functools.partial(run, base * UNIT))


def exchange_kernel(
    n, units, feat, mean, scale, noise, logits, noise_out, held, part_out, part_in,
    send, recv, part_send, part_recv, nsend, nrecv, local, nlocal,
):
    me, cls = lax.axis_index("draw"), lax.axis_index("cls")
    half, rows = n // 2, mean.shape[1]
    mirror = lax.rem(me + half, n)
    base, spot = lax.div(me, half) * half, lax.rem(me, half)
    barrier = pltpu.get_barrier_semaphore()
    for k in range(1, n):
        pl.semaphore_signal(barrier, inc=1, device_id=(cls, lax.rem(me + k, n)), device_id_type=MESH)
    pl.semaphore_wait(barrier, n - 1)

    def remote(source, target, send_sem, recv_sem, device):
        return pltpu.make_async_remote_copy(
            source, target, send_sem, recv_sem, device_id=(cls, device), device_id_type=MESH
        )

    def noise_copy(slot, k, device):
        return remote(noise, noise_out.at[slot], nsend.at[k], nrecv.at[slot], device)

    def block(head, owner, width):
        start = pl.multiple_of(start_of(owner, n, units) * UNIT, UNIT)
        return (mean, scale)[head].at[pl.ds(start, width)]

    def block_copy(far, head, owner, k, source, device, act):
        at_width(
            owner, n, units,
            lambda w: act(
                remote(
                    block(head, owner, w), held.at[far, head, source, pl.ds(0, w)],
                    send.at[far, head, k], recv.at[far, head, source], device,
                )
            ),
        )

    def own_copy(far, head, act):
        owner = mirror if far else me
        at_width(
            owner, n, units,
            lambda w: act(
                pltpu.make_async_copy(
                    block(head, owner, w), held.at[far, head, spot, pl.ds(0, w)], local.at[far, head]
                )
            ),
        )

    def sends(far, head, act):
        for k in range(1, half):
            peer = base + lax.rem(spot + k, half)
            block_copy(far, head, lax.rem(peer + half, n) if far else peer, k, spot, peer, act)

    def columns_of(source):
        if rows % 128:
            return feat[source]
        return feat[:, pl.ds(pl.multiple_of(source * rows, rows), rows)]

    def arrive(far, head):
        owner = mirror if far else me
        for k in range(1, half):
            source = lax.rem(spot + half - k, half)
            block_copy(far, head, owner, k, source, base + source, lambda c: c.wait_recv())
        own_copy(far, head, lambda c: c.wait())
        total = None
        for source in range(half):
            term = lax.dot_general(
                held[far, head, source], columns_of(base + source), (((1,), (1,)), ((), ())),
                preferred_element_type=jnp.float32,
            )
            total = term if total is None else total + term
        return total

    def part_copy(head):
        return remote(part_out.at[head], part_in.at[head], part_send.at[head], part_recv.at[head], mirror)

    own_noise = pltpu.make_async_copy(noise, noise_out.at[me], nlocal)
    stages = [(1, 0), (1, 1), (0, 0), (0, 1)]
    sends(1, 0, lambda c: c.start())
    for k in range(1, n):
        noise_copy(me, k, lax.rem(me + k, n)).start()
    for far, head in stages[1:]:
        sends(far, head, lambda c: c.start())
    for far, head in stages:
        own_copy(far, head, lambda c: c.start())
    own_noise.start()
    for head in range(2):
        part_out[head] = arrive(1, head)
        part_copy(head).start()
    for head in range(2):
        logits[head] = arrive(0, head)
    for k in range(1, n):
        source = lax.rem(me + n - k, n)
        noise_copy(source, k, source).wait_recv()
    own_noise.wait()
    for head in range(2):
        part_copy(head).wait_recv()
        logits[head] = logits[head] + part_in[head]
    for far, head in stages:
        sends(far, head, lambda c: c.wait_send())
    for k in range(1, n):
        noise_copy(me, k, lax.rem(me + k, n)).wait_send()
    for head in range(2):
        part_copy(head).wait_send()


def gather_kernel(n, units, cot, out, send, recv, local):
    me, cls = lax.axis_index("draw"), lax.axis_index("cls")
    half = n // 2
    group, side = lax.div(me, 2), lax.rem(me, 2)
    partner = group * 2 + 1 - side
    split = units // n // 2 * UNIT
    pieces = [(head, part) for head in range(2) for part in range(2)]
    barrier = pltpu.get_barrier_semaphore()
    peers = [partner] + [lax.rem(group + k, half) * 2 + side for k in range(1, half)]
    for peer in peers:
        pl.semaphore_signal(barrier, inc=1, device_id=(cls, peer), device_id_type=MESH)
    pl.semaphore_wait(barrier, half)

    def source(piece, width):
        head, part = pieces[piece]
        return cot.at[head, pl.ds(split, width - split) if part else pl.ds(0, split)]

    def place(piece, owner, width):
        head, part = pieces[piece]
        start = start_of(owner, n, units) * UNIT + part * split
        return out.at[head, pl.ds(pl.multiple_of(start, UNIT), width - split if part else split)]

    def send_own(piece, owner, slot, device, act):
        at_width(
            owner, n, units,
            lambda w: act(
                pltpu.make_async_remote_copy(
                    source(piece, w), place(piece, owner, w), send.at[slot, piece], recv.at[owner, piece],
                    device_id=(cls, device), device_id_type=MESH,
                )
            ),
        )

    def forward(piece, owner, slot, act):
        at_width(
            owner, n, units,
            lambda w: act(
                pltpu.make_async_remote_copy(
                    place(piece, owner, w), place(piece, owner, w), send.at[slot, piece], recv.at[owner, piece],
                    device_id=(cls, partner), device_id_type=MESH,
                )
            ),
        )

    def own(piece, act):
        at_width(
            me, n, units,
            lambda w: act(pltpu.make_async_copy(source(piece, w), place(piece, me, w), local.at[piece])),
        )

    count = len(pieces)
    for piece in range(count):
        for k in range(1, half):
            send_own(piece, me, k, peers[k], lambda c: c.start())
        send_own(piece, me, 0, partner, lambda c: c.start())
    for piece in range(count):
        own(piece, lambda c: c.start())
    order = sorted(range(1, half), key=lambda k: min(k, half - k))
    for piece in range(count):
        for k in order:
            send_own(piece, peers[k], k, peers[k], lambda c: c.wait_recv())
            forward(piece, peers[k], half + k, lambda c: c.start())
    for piece in range(count):
        send_own(piece, partner, 0, partner, lambda c: c.wait_recv())
        for k in range(1, half):
            owner = lax.rem(group + k, half) * 2 + 1 - side
            forward(piece, owner, half + k, lambda c: c.wait_recv())
    for piece in range(count):
        for k in range(half):
            send_own(piece, me, k, peers[k], lambda c: c.wait_send())
        for k in range(1, half):
            forward(piece, peers[k], half + k, lambda c: c.wait_send())
        own(piece, lambda c: c.wait())


def merge(slots, count, softmax):
    if not softmax:
        total = slots[0]
        for i in range(1, count):
            total = total + slots[i]
        return total
    top = slots[0, 0]
    for i in range(1, count):
        top = jnp.maximum(top, slots[i, 0])
    total = jnp.zeros_like(top)
    for i in range(count):
        total = total + slots[i, 1] * jnp.exp(slots[i, 0] - top)
    return jnp.stack((top, total))


def reduce_kernel(counts, softmax, x, out, *scratch):
    levels = len(counts)
    slots, sends, recvs = scratch[:levels], scratch[levels : 2 * levels], scratch[2 * levels :]
    cls, draw = lax.axis_index("cls"), lax.axis_index("draw")

    def device(level, index):
        return (index, draw) if level == 0 else (cls, index)

    barrier = pltpu.get_barrier_semaphore()
    for level, n in enumerate(counts):
        me = (cls, draw)[level]
        for k in range(1, n):
            pl.semaphore_signal(
                barrier, inc=1, device_id=device(level, lax.rem(me + k, n)), device_id_type=MESH
            )
    pl.semaphore_wait(barrier, sum(counts) - levels)
    value = x[...]
    for level, n in enumerate(counts):
        me = (cls, draw)[level]
        held = slots[level]
        held[me] = value

        def copy(slot, k, target):
            return pltpu.make_async_remote_copy(
                held.at[slot], held.at[slot], sends[level].at[k], recvs[level].at[slot],
                device_id=device(level, target), device_id_type=MESH,
            )

        for k in range(1, n):
            copy(me, k, lax.rem(me + k, n)).start()
        for k in range(1, n):
            source = lax.rem(me + n - k, n)
            copy(source, k, source).wait_recv()
        for k in range(1, n):
            copy(me, k, lax.rem(me + k, n)).wait_send()
        value = merge(held, n, softmax)
    if softmax:
        out[...] = value[0] + jnp.log(value[1])
    else:
        out[...] = value


def params(collective_id, grant=32):
    return pltpu.CompilerParams(
        collective_id=collective_id, has_side_effects=True, vmem_limit_bytes=grant * 2**20
    )


def reduce_over(x, counts, softmax, collective_id):
    shape = x.shape[1:] if softmax else x.shape
    return pl.pallas_call(
        functools.partial(reduce_kernel, counts, softmax),
        out_shape=jax.ShapeDtypeStruct(shape, jnp.float32),
        in_specs=[VMEM],
        out_specs=VMEM,
        scratch_shapes=[pltpu.VMEM((n,) + x.shape, jnp.float32) for n in counts]
        + [pltpu.SemaphoreType.DMA((n,)) for n in counts]
        + [pltpu.SemaphoreType.DMA((n,)) for n in counts],
        compiler_params=params(collective_id),
    )(x)


def on_device(features, mean_head, scale_head, factor, noise, labels):
    rows, columns = mean_head.shape
    batch = features.shape[0]
    n, ncls = lax.axis_size("draw"), lax.axis_size("cls")
    me = lax.axis_index("draw")
    units = columns // UNIT
    tile = -(-units // n) * UNIT
    own, rank = noise.shape[0], noise.shape[2]
    draws = own * n
    mean_rows, scale_rows = mean_head.T, scale_head.T
    half = n // 2
    feat = features.reshape(batch, n, rows).transpose(1, 0, 2) if rows % 128 else features

    heads, noise_t = pl.pallas_call(
        functools.partial(exchange_kernel, n, units),
        out_shape=(
            jax.ShapeDtypeStruct((2, tile, batch), jnp.float32),
            jax.ShapeDtypeStruct((n, own, rank, batch), jnp.bfloat16),
        ),
        in_specs=[VMEM] + [ANY] * 3,
        out_specs=(VMEM, ANY),
        scratch_shapes=[
            pltpu.VMEM((2, 2, half, tile, rows), jnp.bfloat16),
            pltpu.VMEM((2, tile, batch), jnp.float32),
            pltpu.VMEM((2, tile, batch), jnp.float32),
            pltpu.SemaphoreType.DMA((2, 2, half)),
            pltpu.SemaphoreType.DMA((2, 2, half)),
            pltpu.SemaphoreType.DMA((2,)),
            pltpu.SemaphoreType.DMA((2,)),
            pltpu.SemaphoreType.DMA((n,)),
            pltpu.SemaphoreType.DMA((n,)),
            pltpu.SemaphoreType.DMA((2, 2)),
            pltpu.SemaphoreType.DMA,
        ],
        compiler_params=params(0),
    )(feat, mean_rows, scale_rows, noise.transpose(0, 2, 1))

    first = start_of(me, n, units) * UNIT
    width = start_of(me + 1, n, units) * UNIT - first
    offsets = jnp.arange(tile, dtype=jnp.int32)[:, None]
    valid = offsets < width
    class_ids = lax.axis_index("cls") * columns + first + offsets
    shift = jnp.where(class_ids >= CREAL, 30000.0, 0.0).astype(jnp.float32)
    my_factor = lax.dynamic_slice_in_dim(factor.T, first, tile, 1)
    my_labels = jnp.where(valid, lax.dynamic_slice_in_dim(labels.T, first, tile, 0), 0.0)

    mean_logit, scale_pre = heads[0], heads[1]
    scale_pre = jnp.where(valid, scale_pre, 0.0)
    spread = jax.nn.softplus(scale_pre)
    lowrank = jnp.einsum(
        "rc,srb->scb", my_factor, noise_t.reshape(draws, rank, batch), preferred_element_type=jnp.float32
    )
    logits = mean_logit[None] + spread[None] * lowrank - shift[None]
    logits = jnp.where(valid[None], logits, -1e30)
    local_top = jnp.max(logits, axis=1)
    local_total = jnp.sum(jnp.exp(logits - local_top[:, None]), axis=1)
    lse = reduce_over(jnp.stack((local_top, local_total)), (ncls, n), True, 1)
    log_prob = logits - lse[:, None]
    best = jnp.max(log_prob, axis=0)
    risen = jnp.exp(log_prob - best[None])
    inverse = 1.0 / jnp.sum(risen, axis=0)
    weight = my_labels * inverse
    label_dot = reduce_over(jnp.sum(weight[None] * risen, axis=1), (ncls, n), False, 2)
    logit_cot = risen * ((jnp.exp(best) / batch)[None] * label_dot[:, None] - (weight / batch)[None])
    dmean = jnp.sum(logit_cot, axis=0)
    dspread = jnp.sum(logit_cot * lowrank, axis=0)
    cots = jnp.stack((dmean, dspread * jax.nn.sigmoid(scale_pre))).astype(jnp.bfloat16)

    gathered = pl.pallas_call(
        functools.partial(gather_kernel, n, units),
        out_shape=jax.ShapeDtypeStruct((2, columns, batch), jnp.bfloat16),
        in_specs=[ANY],
        out_specs=ANY,
        scratch_shapes=[
            pltpu.SemaphoreType.DMA((n, 4)),
            pltpu.SemaphoreType.DMA((n, 4)),
            pltpu.SemaphoreType.DMA((4,)),
        ],
        compiler_params=params(3),
    )(cots)
    mean_cot, scale_cot = gathered[0], gathered[1]
    my_columns = lax.dynamic_slice_in_dim(features, me * rows, rows, 1)
    over_classes = (((0,), (0,)), ((), ()))
    feature_part = lax.dot_general(
        mean_cot, mean_rows, over_classes, preferred_element_type=jnp.float32
    ) + lax.dot_general(scale_cot, scale_rows, over_classes, preferred_element_type=jnp.float32)
    mean_grad = jnp.dot(mean_cot, my_columns, preferred_element_type=jnp.float32).T
    scale_grad = jnp.dot(scale_cot, my_columns, preferred_element_type=jnp.float32).T
    feature_grad, step = feature_part, 1
    while step < ncls:
        feature_grad = feature_grad + lax.ppermute(feature_grad, "cls", [(i, i ^ step) for i in range(ncls)])
        step *= 2
    return (mean_grad, scale_grad, feature_grad)


def solution(mesh):
    return jax.shard_map(
        on_device,
        mesh=mesh,
        in_specs=(
            P(),
            P("draw", "cls"),
            P("draw", "cls"),
            P("cls", None),
            P("draw", None, None),
            P(None, "cls"),
        ),
        out_specs=(P("draw", "cls"), P("draw", "cls"), P(None, "draw")),
        check_vma=False,
    )
```
